32 devices in a mesh: row: 8 (over z, x), col: 4 (over y, core).
Axes of the slice: x: 2, y: 2, z: 4, core: 2. Of those that a mesh axis runs over, the one named last changes fastest.
Arguments:
- coeff: bfloat16 [8192, 512], P('row'), may hold values from -6 to 6
- tri_blocks: bfloat16 [5120, 256, 128], P(('row', 'col')), may hold values from -0.0390625 to 0.0390625
- pair_aux: int32 [5120], P(('row', 'col')), may hold values from 0 to 7
- pair_ao: int32 [5120], P(('row', 'col')), may hold values from 0 to 7
- owner_slot: int32 [4, 8], P('col'), may hold values from 0 to 15, as said below
- metric_blocks: bfloat16 [2048, 128, 128], P(('row', 'col')), may hold values from -0.125 to 0.125
- pair_slot: int32 [2048], P(('row', 'col')), may hold values from 0 to 1
- pair_out: int32 [2048], P(('row', 'col')), may hold values from 0 to 7
Outputs:
- transformed: bfloat16 [8192, 1024], P(('row', 'col'))
The draws below stay inside these ranges and needn't reach their ends.
Inputs may be any that keep to these rules, and one draw needn't show every extreme that they name: `owner_slot`: within a column the 8 entries are distinct slots; slot s belongs to row s // 2; in every column some row receives 2 blocks.
All inputs are finite; a program needn't handle non-finite values.
Results may differ from the reference program's by a relative error of at most 0.014.
Values may be sent and summed in bfloat16 or wider, within the bound.
No kernel may reach another device: no remote copies, remote signals or barrier semaphores. Data moves between devices by JAX's collectives and lax.ppermute only.
A program may use at most 128 MiB of HBM per device.

```python
import math
import jax
import jax.numpy as jnp
from jax import lax

BLOCK = 128
OCC = 512
NUW = 2
AOB_DEV = 8
MAXOWN = 2
PPA = 20
PB_COL = 8
NB1 = 160
QB_DEV = 2
NB2 = 64
AO_BLOCKS = 64
N_ROW = 8
N_COL = 4


def draw_owner_slot(key, part):
    total = N_ROW * MAXOWN

    def one_column(column):
        column_key = jax.random.fold_in(key, column)
        shuffled = jax.random.permutation(jax.random.fold_in(column_key, 1), total)
        chosen = jax.random.randint(jax.random.fold_in(column_key, 2), (), 0, N_ROW)
        slots = jnp.arange(total, dtype=jnp.int32)
        ends = jnp.logical_or(slots == 0, slots == total - 1).astype(jnp.int32)
        scores = shuffled.astype(jnp.int32) - total * (slots // MAXOWN == chosen).astype(jnp.int32) - 2 * total * ends
        ordering = jnp.argsort(scores, stable=True)
        return ordering[:PB_COL].astype(jnp.int32)
    return jax.vmap(one_column)(jnp.arange(N_COL, dtype=jnp.int32))


def touch_ends(entries, key, smallest, high):
    place = [jax.random.randint(jax.random.fold_in(key, axis), (), 0, length) for axis, length in enumerate(entries.shape)]
    main_axis = entries.shape.index(max(entries.shape))
    next_to = place[:main_axis] + [(place[main_axis] + 1) % entries.shape[main_axis]] + place[main_axis + 1:]
    return entries.at[tuple(place)].set(smallest).at[tuple(next_to)].set(high)


def shard_levels(own_key, extent, shards, least, high):
    level, own = 1.0, jax.random.fold_in(own_key, 6)
    for position, blocks in shards:
        steps = jnp.exp(jax.random.uniform(jax.random.fold_in(own, position), (blocks,), jnp.float32, least / len(shards), high / len(shards)))
        level = level * jnp.repeat(steps, extent[position] // blocks).reshape([-1 if axis == position else 1 for axis in range(len(extent))])
    return level


def scatter_about(stream_key, dims, scale, most, shards=(), held_as=jnp.bfloat16):
    level = shard_levels(stream_key, dims, shards, -0.22, 0.18) if shards else 1.0
    entries = jax.random.normal(stream_key, dims, jnp.float32) * scale * level
    return jnp.minimum(jnp.maximum(entries, -most), most).astype(held_as)


def setup_inputs(seed: int = 0) -> dict:
    streams_of = jax.random.split(jax.random.key(seed), 9)
    coeff = scatter_about(streams_of[0], (AO_BLOCKS * BLOCK, OCC), 1.0, 6.0, ((0, 8),))
    tri_blocks = scatter_about(streams_of[1], (N_ROW * N_COL * NB1, BLOCK * NUW, BLOCK), (N_ROW * PPA * BLOCK) ** -0.5, 0.0390625, ((0, 32),))
    pair_aux = touch_ends(jax.random.randint(streams_of[2], (N_ROW * N_COL * NB1,), 0, PB_COL), jax.random.fold_in(streams_of[2], 1), 0, PB_COL - 1).astype(jnp.int32)
    pair_ao = touch_ends(jax.random.randint(streams_of[3], (N_ROW * N_COL * NB1,), 0, AOB_DEV), jax.random.fold_in(streams_of[3], 1), 0, AOB_DEV - 1).astype(jnp.int32)
    owner_slot = draw_owner_slot(jax.random.fold_in(streams_of[8], 71), 0)
    metric_blocks = scatter_about(streams_of[5], (N_ROW * N_COL * NB2, BLOCK, BLOCK), (BLOCK * NB2 // (2 * QB_DEV)) ** -0.5, 0.125, ((0, 32),))
    pair_slot = touch_ends(jax.random.randint(streams_of[6], (N_ROW * N_COL * NB2,), 0, MAXOWN), jax.random.fold_in(streams_of[6], 1), 0, MAXOWN - 1).astype(jnp.int32)
    pair_out = touch_ends(jax.random.randint(streams_of[7], (N_ROW * N_COL * NB2,), 0, N_COL * QB_DEV), jax.random.fold_in(streams_of[7], 1), 0, (N_COL * QB_DEV) - 1).astype(jnp.int32)
    return {"coeff": coeff, "tri_blocks": tri_blocks, "pair_aux": pair_aux, "pair_ao": pair_ao, "owner_slot": owner_slot, "metric_blocks": metric_blocks, "pair_slot": pair_slot, "pair_out": pair_out}


def first_section(tiles, aux_ids, ao_ids, coeff_blocks):
    count = tiles.shape[0]
    group_size = math.gcd(count, 32)
    width = NUW * OCC
    tile_sets = tiles.reshape(count // group_size, group_size, BLOCK * NUW, BLOCK)
    aux_sets = aux_ids.reshape(count // group_size, group_size)
    ao_sets = ao_ids.reshape(count // group_size, group_size)

    def advance(total, pieces):
        tile_set, aux_set, ao_set = pieces
        gathered = coeff_blocks[ao_set]
        products = jnp.einsum("kab,kbo->kao", tile_set.astype(jnp.float32), gathered.astype(jnp.float32))
        products = products.reshape(group_size, BLOCK, width)
        return total + jax.ops.segment_sum(products, aux_set, num_segments=PB_COL), None

    start = jnp.zeros((PB_COL, BLOCK, width), jnp.float32)
    total, unused = lax.scan(advance, start, (tile_sets, aux_sets, ao_sets))
    return total


def second_section(metric, slot_ids, out_ids, owned):
    count = metric.shape[0]
    group_size = math.gcd(count, 32)
    width = NUW * OCC
    metric_sets = metric.reshape(count // group_size, group_size, BLOCK, BLOCK)
    slot_sets = slot_ids.reshape(count // group_size, group_size)
    out_sets = out_ids.reshape(count // group_size, group_size)

    def advance(total, pieces):
        metric_set, slot_set, out_set = pieces
        gathered = owned[slot_set]
        products = jnp.einsum("kab,kbw->kaw", metric_set.astype(jnp.float32), gathered.astype(jnp.float32))
        return total + jax.ops.segment_sum(products, out_set, num_segments=N_COL * QB_DEV), None

    start = jnp.zeros((N_COL * QB_DEV, BLOCK, width), jnp.float32)
    total, unused = lax.scan(advance, start, (metric_sets, slot_sets, out_sets))
    return total


def reference(coeff, tri_blocks, pair_aux, pair_ao, owner_slot, metric_blocks, pair_slot, pair_out):
    width = NUW * OCC
    coeff_rows = coeff.reshape(N_ROW, AOB_DEV, BLOCK, OCC)
    tiles = tri_blocks.reshape(N_ROW, N_COL, NB1, BLOCK * NUW, BLOCK)
    aux_all = pair_aux.reshape(N_ROW, N_COL, NB1)
    ao_all = pair_ao.reshape(N_ROW, N_COL, NB1)
    metric = metric_blocks.reshape(N_ROW, N_COL, NB2, BLOCK, BLOCK)
    slot_all = pair_slot.reshape(N_ROW, N_COL, NB2)
    out_all = pair_out.reshape(N_ROW, N_COL, NB2)

    def per_column(column, outputs):
        def add_row(row, summed):
            partial_value = first_section(tiles[row, column], aux_all[row, column], ao_all[row, column], coeff_rows[row])
            rounded = lax.optimization_barrier(partial_value.astype(jnp.bfloat16))
            return summed + rounded.astype(jnp.float32)

        summed = lax.fori_loop(0, N_ROW, add_row, jnp.zeros((PB_COL, BLOCK, width), jnp.float32))
        placed = jnp.zeros((N_ROW * MAXOWN, BLOCK, width), jnp.bfloat16)
        placed = placed.at[owner_slot[column]].set(summed.astype(jnp.bfloat16))
        placed = placed.reshape(N_ROW, MAXOWN, BLOCK, width)

        def add_out(row, current):
            term = second_section(metric[row, column], slot_all[row, column], out_all[row, column], placed[row])
            rounded = lax.optimization_barrier(term.astype(jnp.bfloat16))
            return current.at[row].add(rounded.astype(jnp.float32))

        return lax.fori_loop(0, N_ROW, add_out, outputs)

    outputs = lax.fori_loop(0, N_COL, per_column, jnp.zeros((N_ROW, N_COL * QB_DEV, BLOCK, width), jnp.float32))
    return outputs.astype(jnp.bfloat16).reshape(N_ROW * N_COL * QB_DEV * BLOCK, width)
```

```python
import functools
import math

import jax
import jax.numpy as jnp
from jax import lax
from jax.experimental import pallas as pl
from jax.experimental.pallas import tpu as pltpu
from jax.sharding import PartitionSpec as P

BLOCK = 128
OCC = 512
NUW = 2
WIDTH = NUW * OCC
MAXOWN = 2
QB_DEV = 2
PIECES = 2
VMEM_BYTES = 48 << 20


def smem():
    return pl.BlockSpec(memory_space=pltpu.SMEM)


def vmem():
    return pl.BlockSpec(memory_space=pltpu.VMEM)


def params():
    return pltpu.CompilerParams(vmem_limit_bytes=VMEM_BYTES)


def cost(flops, moved):
    return pl.CostEstimate(flops=int(flops), bytes_accessed=int(moved), transcendentals=0)


def write_plan(rows, owner, plan, occ, order, place, moved_flag, start):
    pairs = rows // 2
    i32 = jnp.int32
    for s in range(2 * rows):
        occ[s] = i32(-1)
    for j in range(rows):
        occ[owner[0, j]] = i32(j)
    held = [occ[s] for s in range(2 * rows)]
    has = [(h >= 0).astype(i32) for h in held]
    first_side = sum(has[4 * z] + has[4 * z + 1] for z in range(pairs))
    giver = jnp.where(first_side > pairs, i32(0), i32(1))
    need = jnp.abs(first_side - pairs)
    moved = i32(0)
    counts = [i32(0), i32(0)]
    for z in range(pairs):
        n0 = has[4 * z] + has[4 * z + 1]
        n1 = has[4 * z + 2] + has[4 * z + 3]
        from_count = jnp.where(giver == 0, n0, n1)
        to_count = n0 + n1 - from_count
        move = jnp.logical_and(moved < need, jnp.logical_and(from_count >= 1, to_count <= 1)).astype(i32)
        moved = moved + move
        start[z] = counts[0]
        start[pairs + z] = counts[1]
        for x in range(2):
            for parity in range(2):
                s = 4 * z + 2 * x + parity
                pick = has[s] if parity else has[s] * (1 - has[s + 1])
                chosen = move * pick * jnp.where(giver == x, i32(1), i32(0))
                side = jnp.where(chosen == 1, i32(1 - x), i32(x))
                spot = jnp.where(side == 0, counts[0], counts[1])
                order[jnp.where(has[s] == 1, side * pairs + spot, i32(2 * pairs))] = held[s]
                place[s] = jnp.where(has[s] == 1, spot, i32(-1))
                moved_flag[s] = chosen
                counts[0] = counts[0] + has[s] * (1 - side)
                counts[1] = counts[1] + has[s] * side
    row = lax.axis_index("row")
    z, x = row // 2, row % 2
    lower = z < pairs // 2
    window = jnp.where(lower, 2 * (z + 1), 2 * (pairs - z))
    offset = jnp.where(lower, 0, pairs - window)
    base = jnp.minimum(start[x * pairs + z] - offset, window - 2)
    plan[0] = base
    away = i32(0)
    for parity in range(2):
        s = 4 * z + 2 * (1 - x) + parity
        away = jnp.where(moved_flag[s] == 1, place[s] - offset - base, away)
    plan[1] = away
    for parity in range(2):
        s = 2 * row + parity
        where = jnp.where(moved_flag[s] == 1, i32(2), place[s] - offset - base)
        plan[2 + parity] = jnp.where(place[s] >= 0, where, i32(3))


def first_kernel(rows, table, group, pieces, aux, ao, owner, tiles, coeff, *rest):
    outs, plan = rest[: 2 * pieces], rest[2 * pieces]
    dense, occ, order, place, moved_flag, start = rest[2 * pieces + 1 :]
    pairs = rows // 2
    step = pl.program_id(0)

    @pl.when(step == 0)
    def _():
        write_plan(rows, owner, plan, occ, order, place, moved_flag, start)

        @pl.loop(0, rows * table)
        def _(k):
            dense[k] = jnp.zeros((NUW * BLOCK, BLOCK), jnp.float32)

    @pl.loop(0, group)
    def _(t):
        k = step * group + t
        where = aux[k] * table + ao[k]
        dense[where] += tiles[t].astype(jnp.float32)

    @pl.when(step == pl.num_programs(0) - 1)
    def _():
        x = lax.axis_index("row") % 2
        span = WIDTH // pieces
        for part in range(2):
            side = x if part == 0 else 1 - x

            @pl.loop(0, pairs // 2)
            def _(p):
                for nu in range(NUW):
                    blocks = []
                    for h in range(2):
                        j = order[side * pairs + 2 * p + h]
                        blocks.append(
                            jnp.concatenate(
                                [
                                    dense[j * table + a, pl.ds(nu, BLOCK, stride=NUW), :].astype(jnp.bfloat16)
                                    for a in range(table)
                                ],
                                axis=1,
                            )
                        )
                    left = jnp.concatenate(blocks, axis=0)
                    made = jnp.dot(left, coeff[...], preferred_element_type=jnp.float32).astype(jnp.bfloat16)
                    for h in range(2):
                        for column in range(nu * OCC, (nu + 1) * OCC, min(span, OCC)):
                            piece, inner = column // span, column % span
                            size = min(span, OCC)
                            at = column - nu * OCC
                            outs[2 * piece + part][2 * p + h, :, inner : inner + size] = made[
                                h * BLOCK : (h + 1) * BLOCK, at : at + size
                            ]


def first_section(tiles, aux, ao, owner, coeff, rows, pieces):
    count = tiles.shape[0]
    table = coeff.shape[0] // BLOCK
    group = math.gcd(count, 20)
    pairs = rows // 2
    span = WIDTH // pieces
    piece_shape = jax.ShapeDtypeStruct((pairs, BLOCK, span), jnp.bfloat16)
    whole = pl.BlockSpec((pairs, BLOCK, span), lambda g, *_: (0, 0, 0))
    return pl.pallas_call(
        functools.partial(first_kernel, rows, table, group, pieces),
        grid_spec=pltpu.PrefetchScalarGridSpec(
            num_scalar_prefetch=3,
            grid=(count // group,),
            in_specs=[
                pl.BlockSpec((group, NUW * BLOCK, BLOCK), lambda g, *_: (g, 0, 0)),
                pl.BlockSpec((coeff.shape[0], OCC), lambda g, *_: (0, 0)),
            ],
            out_specs=[whole] * (2 * pieces) + [smem()],
            scratch_shapes=[
                pltpu.VMEM((rows * table, NUW * BLOCK, BLOCK), jnp.float32),
                pltpu.SMEM((2 * rows,), jnp.int32),
                pltpu.SMEM((2 * pairs + 1,), jnp.int32),
                pltpu.SMEM((2 * rows,), jnp.int32),
                pltpu.SMEM((2 * rows,), jnp.int32),
                pltpu.SMEM((2 * pairs,), jnp.int32),
            ],
        ),
        out_shape=[piece_shape] * (2 * pieces) + [jax.ShapeDtypeStruct((4,), jnp.int32)],
        compiler_params=params(),
        cost_estimate=cost(2 * rows * NUW * BLOCK * table * BLOCK * OCC, tiles.size * 2 + coeff.size * 2),
        name="first_section",
    )(aux, ao, owner, tiles, coeff)


def metric_kernel(ys, plan, slots, outs_of, metric, keep, send, dense):
    col = lax.axis_index("col")
    y, core = col // 2, col % 2

    @pl.loop(0, dense.shape[0])
    def _(k):
        dense[k] = jnp.zeros((BLOCK, BLOCK), jnp.float32)

    @pl.loop(0, metric.shape[0])
    def _(k):
        where = outs_of[k] * 4 + plan[2 + slots[k]]
        dense[where] += metric[k].astype(jnp.float32)

    for target, mine in ((keep, core), (send, 1 - core)):
        for d in range(ys):
            to_col = lax.rem(y + d, ys) * 2 + mine
            for h in range(QB_DEV):
                for spot in range(3):
                    target[d, h * BLOCK : (h + 1) * BLOCK, spot * BLOCK : (spot + 1) * BLOCK] = dense[
                        (to_col * QB_DEV + h) * 4 + spot
                    ].astype(jnp.bfloat16)


def metric_section(plan, slots, outs_of, metric, cols):
    ys = cols // 2
    shape = jax.ShapeDtypeStruct((ys, QB_DEV * BLOCK, 3 * BLOCK), jnp.bfloat16)
    return pl.pallas_call(
        functools.partial(metric_kernel, ys),
        in_specs=[smem(), smem(), smem(), vmem()],
        out_specs=[vmem(), vmem()],
        out_shape=[shape, shape],
        scratch_shapes=[pltpu.VMEM((cols * QB_DEV * 4, BLOCK, BLOCK), jnp.float32)],
        compiler_params=params(),
        cost_estimate=cost(0, metric.size * 2 + cols * 400000),
        name="metric_section",
    )(plan, slots, outs_of, metric)


def middle_kernel(pairs, plan, mine, other, own, outward):
    def total(k):
        return (mine[k].astype(jnp.float32) + other[k].astype(jnp.float32)).astype(jnp.bfloat16)

    shift = jnp.where(lax.axis_index("row") // 2 < pairs // 2, 0, 2)
    base = plan[0]
    for k in range(2):
        own[k] = total(base + k)
    for k in range(pairs - 2):
        outward[k] = total(shift + k)


def middle_section(plan, mine, other):
    pairs, _, span = mine.shape
    return pl.pallas_call(
        functools.partial(middle_kernel, pairs),
        in_specs=[smem(), vmem(), vmem()],
        out_specs=[vmem(), vmem()],
        out_shape=[
            jax.ShapeDtypeStruct((2, BLOCK, span), jnp.bfloat16),
            jax.ShapeDtypeStruct((pairs - 2, BLOCK, span), jnp.bfloat16),
        ],
        compiler_params=params(),
        cost_estimate=cost(mine.size, mine.size * 6),
        name="middle_section",
    )(plan, mine, other)


def outward_kernel(pairs, level, plan, own, came, own_out, rest):
    z = lax.axis_index("row") // 2
    lower = z < pairs // 2
    distance = jnp.where(lower, pairs // 2 - 1 - z, z - pairs // 2)
    here = distance == level
    base = plan[0]

    @pl.when(here)
    def _():
        for k in range(2):
            own_out[k] = came[base + k]

    @pl.when(jnp.logical_not(here))
    def _():
        for k in range(2):
            own_out[k] = own[k]

    if level == pairs // 2 - 1:
        rest[0] = own_out[plan[1]]
    else:
        shift = jnp.where(lower, 0, 2)
        for k in range(rest.shape[0]):
            rest[k] = came[shift + k]


def outward_section(plan, own, came, level, pairs):
    span = own.shape[2]
    last = level == pairs // 2 - 1
    return pl.pallas_call(
        functools.partial(outward_kernel, pairs, level),
        in_specs=[smem(), vmem(), vmem()],
        out_specs=[vmem(), vmem()],
        out_shape=[
            jax.ShapeDtypeStruct((2, BLOCK, span), jnp.bfloat16),
            jax.ShapeDtypeStruct((1 if last else came.shape[0] - 2, BLOCK, span), jnp.bfloat16),
        ],
        compiler_params=params(),
        cost_estimate=cost(0, own.size * 8),
        name="outward_section",
    )(plan, own, came)


def term_kernel(ys, keep, got, own, own_core, fix, fix_core, sent, kept):
    span = own.shape[2]
    right = jnp.concatenate(
        [
            own[...].reshape(2 * BLOCK, span),
            fix[0],
            own_core[...].reshape(2 * BLOCK, span),
            fix_core[0],
        ],
        axis=0,
    )
    for d in range(ys - 1, -1, -1):
        left = jnp.concatenate([keep[d], got[d]], axis=1)
        made = jnp.dot(left, right, preferred_element_type=jnp.float32)
        if d:
            sent[d - 1] = made.astype(jnp.bfloat16)
        else:
            kept[...] = made


def term_section(keep, got, own, own_core, fix, fix_core):
    ys = keep.shape[0]
    span = own.shape[2]
    return pl.pallas_call(
        functools.partial(term_kernel, ys),
        in_specs=[vmem()] * 6,
        out_specs=[vmem(), vmem()],
        out_shape=[
            jax.ShapeDtypeStruct((ys - 1, QB_DEV * BLOCK, span), jnp.bfloat16),
            jax.ShapeDtypeStruct((QB_DEV * BLOCK, span), jnp.float32),
        ],
        compiler_params=params(),
        cost_estimate=cost(2 * ys * QB_DEV * BLOCK * 6 * BLOCK * span, keep.size * 4 + span * BLOCK * 24),
        name="term_section",
    )(keep, got, own, own_core, fix, fix_core)


def added(a, b):
    return (a.astype(jnp.float32) + b.astype(jnp.float32)).astype(jnp.bfloat16)


def per_device(
    coeff, tri_blocks, pair_aux, pair_ao, owner_slot, metric_blocks, pair_slot, pair_out
):
    rows = lax.axis_size("row")
    cols = lax.axis_size("col")
    pairs, ys = rows // 2, cols // 2
    half = pairs // 2

    def on_line(moves):
        return [(2 * a + x, 2 * b + x) for a, b in moves for x in range(2)]

    swap_pair = [(r, r ^ 1) for r in range(rows)]
    swap_core = [(c, c ^ 1) for c in range(cols)]

    made = first_section(tri_blocks, pair_aux, pair_ao, owner_slot, coeff, rows, PIECES)
    plan = made[-1]
    keep, send = metric_section(plan, pair_slot, pair_out, metric_blocks, cols)
    got = lax.ppermute(send, "col", swap_core)

    finished = []
    for piece in range(PIECES):
        total = added(made[2 * piece], lax.ppermute(made[2 * piece + 1], "row", swap_pair))
        for a in range(half - 1):
            inward = on_line([(a, a + 1), (pairs - 1 - a, pairs - 2 - a)])
            total = added(total, lax.ppermute(total, "row", inward))
        other = lax.ppermute(total, "row", on_line([(half - 1, half), (half, half - 1)]))
        own, rest = middle_section(plan, total, other)
        for level in range(1, half):
            outward = on_line([(half - level, half - 1 - level), (half - 1 + level, half + level)])
            own, rest = outward_section(plan, own, lax.ppermute(rest, "row", outward), level, pairs)
        fix = lax.ppermute(rest, "row", swap_pair)
        own_core = lax.ppermute(own, "col", swap_core)
        fix_core = lax.ppermute(fix, "col", swap_core)
        sent, kept = term_section(keep, got, own, own_core, fix, fix_core)
        for d in range(1, ys):
            around = [(2 * y + k, 2 * ((y + d) % ys) + k) for y in range(ys) for k in range(2)]
            kept = kept + lax.ppermute(sent[d - 1], "col", around).astype(jnp.float32)
        finished.append(kept.astype(jnp.bfloat16))
    return jnp.concatenate(finished, axis=1)


def solution(mesh):
    in_specs = (
        P("row", None),
        P(("row", "col"), None, None),
        P(("row", "col")),
        P(("row", "col")),
        P("col", None),
        P(("row", "col"), None, None),
        P(("row", "col")),
        P(("row", "col")),
    )
    out_specs = P(("row", "col"), None)
    return jax.shard_map(
        per_device, mesh=mesh, in_specs=in_specs, out_specs=out_specs, check_vma=False
    )
```

```python
import functools
import math

import jax
import jax.numpy as jnp
from jax import lax
from jax.experimental import pallas as pl
from jax.experimental.pallas import tpu as pltpu
from jax.sharding import PartitionSpec as P

BLOCK = 128
OCC = 512
NUW = 2
MAXOWN = 2
QB_DEV = 2
SMALL_VMEM = 8 << 20


def smem():
    return pl.BlockSpec(memory_space=pltpu.SMEM)


def vmem():
    return pl.BlockSpec(memory_space=pltpu.VMEM)


def params(limit=SMALL_VMEM):
    return pltpu.CompilerParams(vmem_limit_bytes=limit)


def cost(flops, moved):
    return pl.CostEstimate(flops=int(flops), bytes_accessed=int(moved), transcendentals=0)


def write_plan(rows, owner, plan, occ, order, place, moved_flag, start):
    pairs = rows // 2
    i32 = jnp.int32
    for s in range(2 * rows):
        occ[s] = i32(-1)
    for j in range(rows):
        occ[owner[0, j]] = i32(j)
    held = [occ[s] for s in range(2 * rows)]
    has = [(h >= 0).astype(i32) for h in held]
    first_side = sum(has[4 * z] + has[4 * z + 1] for z in range(pairs))
    giver = jnp.where(first_side > pairs, i32(0), i32(1))
    need = jnp.abs(first_side - pairs)
    moved = i32(0)
    counts = [i32(0), i32(0)]
    for z in range(pairs):
        n0 = has[4 * z] + has[4 * z + 1]
        n1 = has[4 * z + 2] + has[4 * z + 3]
        from_count = jnp.where(giver == 0, n0, n1)
        to_count = n0 + n1 - from_count
        move = jnp.logical_and(moved < need, jnp.logical_and(from_count >= 1, to_count <= 1)).astype(i32)
        moved = moved + move
        start[z] = counts[0]
        start[pairs + z] = counts[1]
        for x in range(2):
            for parity in range(2):
                s = 4 * z + 2 * x + parity
                pick = has[s] if parity else has[s] * (1 - has[s + 1])
                chosen = move * pick * jnp.where(giver == x, i32(1), i32(0))
                side = jnp.where(chosen == 1, i32(1 - x), i32(x))
                spot = jnp.where(side == 0, counts[0], counts[1])
                order[jnp.where(has[s] == 1, side * pairs + spot, i32(2 * pairs))] = held[s]
                place[s] = jnp.where(has[s] == 1, spot, i32(-1))
                moved_flag[s] = chosen
                counts[0] = counts[0] + has[s] * (1 - side)
                counts[1] = counts[1] + has[s] * side
    row = lax.axis_index("row")
    z, x = row // 2, row % 2
    lower = z < pairs // 2
    window = jnp.where(lower, 2 * (z + 1), 2 * (pairs - z))
    offset = jnp.where(lower, 0, pairs - window)
    base = jnp.minimum(start[x * pairs + z] - offset, window - 2)
    plan[0] = base
    away = i32(0)
    for parity in range(2):
        s = 4 * z + 2 * (1 - x) + parity
        away = jnp.where(moved_flag[s] == 1, place[s] - offset - base, away)
    plan[1] = away
    for parity in range(2):
        s = 2 * row + parity
        where = jnp.where(moved_flag[s] == 1, i32(2), place[s] - offset - base)
        plan[2 + parity] = jnp.where(place[s] >= 0, where, i32(3))


def first_kernel(
    rows, table, group, aux_in, ao_in, owner_in, tiles_in, coeff_in, keep, send, plan, later,
    tiles, coeff, dense, made, left_later, aux, ao, owner, occ, order, place, moved_flag, start, sems, out_sems,
):
    pairs = rows // 2
    groups = tiles.shape[0]
    small = [
        pltpu.make_async_copy(aux_in, aux, sems.at[groups]),
        pltpu.make_async_copy(ao_in, ao, sems.at[groups + 1]),
        pltpu.make_async_copy(owner_in, owner, sems.at[groups + 2]),
    ]
    loads = [
        pltpu.make_async_copy(tiles_in.at[pl.ds(g * group, group)], tiles.at[g], sems.at[g]) for g in range(groups)
    ]
    table_load = pltpu.make_async_copy(coeff_in, coeff, sems.at[groups + 3])
    for copy in (*small, *loads, table_load):
        copy.start()

    @pl.loop(0, rows * table, unroll=4)
    def _(k):
        dense[k] = jnp.zeros((NUW * BLOCK, BLOCK), jnp.float32)

    for copy in small:
        copy.wait()
    write_plan(rows, owner, plan, occ, order, place, moved_flag, start)

    for g in range(groups):
        loads[g].wait()

        @pl.loop(0, group, unroll=4)
        def _(t):
            k = g * group + t
            where = aux[k] * table + ao[k]
            dense[where] += tiles[g, t].astype(jnp.float32)

    table_load.wait()
    x = lax.axis_index("row") % 2
    stores = []
    for part, out in ((1, send), (0, keep)):
        side = x if part == 0 else 1 - x
        for p in range(pairs // 2):
            at = part * pairs + 2 * p
            for nu in range(NUW):
                blocks = []
                for h in range(2):
                    j = order[side * pairs + 2 * p + h]
                    blocks.append(
                        jnp.concatenate(
                            [
                                dense[j * table + a, pl.ds(nu, BLOCK, stride=NUW), :].astype(jnp.bfloat16)
                                for a in range(table)
                            ],
                            axis=1,
                        )
                    )
                left = jnp.concatenate(blocks, axis=0)
                if nu:
                    left_later[at : at + 2] = left.reshape(2, BLOCK, table * BLOCK)
                    stores.append((left_later.at[pl.ds(at, 2)], later.at[pl.ds(at, 2)]))
                else:
                    value = jnp.dot(left, coeff[...], preferred_element_type=jnp.float32)
                    made[at : at + 2] = value.astype(jnp.bfloat16).reshape(2, BLOCK, OCC)
                    stores.append((made.at[pl.ds(at, 2)], out.at[pl.ds(2 * p, 2)]))
                stores[-1] = pltpu.make_async_copy(*stores[-1], out_sems.at[len(stores) - 1])
                stores[-1].start()
    for copy in stores:
        copy.wait()


def first_section(tiles, aux, ao, owner, coeff, rows):
    count = tiles.shape[0]
    table = coeff.shape[0] // BLOCK
    group = math.gcd(count, 20)
    groups = count // group
    pairs = rows // 2
    any_space = pl.BlockSpec(memory_space=pl.ANY)
    half = jax.ShapeDtypeStruct((pairs, BLOCK, OCC), jnp.bfloat16)
    held = 2 * tiles.size + 2 * coeff.size + rows * table * NUW * BLOCK * BLOCK * 4 + rows * BLOCK * 4 * OCC * 2
    return pl.pallas_call(
        functools.partial(first_kernel, rows, table, group),
        in_specs=[any_space] * 5,
        out_specs=[any_space, any_space, smem(), any_space],
        out_shape=[
            half,
            half,
            jax.ShapeDtypeStruct((4 + pairs,), jnp.int32),
            jax.ShapeDtypeStruct((rows, BLOCK, table * BLOCK), jnp.bfloat16),
        ],
        scratch_shapes=[
            pltpu.VMEM((groups, group, NUW * BLOCK, BLOCK), jnp.bfloat16),
            pltpu.VMEM(coeff.shape, jnp.bfloat16),
            pltpu.VMEM((rows * table, NUW * BLOCK, BLOCK), jnp.float32),
            pltpu.VMEM((rows, BLOCK, OCC), jnp.bfloat16),
            pltpu.VMEM((rows, BLOCK, table * BLOCK), jnp.bfloat16),
            pltpu.SMEM((count,), jnp.int32),
            pltpu.SMEM((count,), jnp.int32),
            pltpu.SMEM(owner.shape, jnp.int32),
            pltpu.SMEM((2 * rows,), jnp.int32),
            pltpu.SMEM((2 * pairs + 1,), jnp.int32),
            pltpu.SMEM((2 * rows,), jnp.int32),
            pltpu.SMEM((2 * rows,), jnp.int32),
            pltpu.SMEM((2 * pairs,), jnp.int32),
            pltpu.SemaphoreType.DMA((groups + 4,)),
            pltpu.SemaphoreType.DMA((NUW * pairs,)),
        ],
        compiler_params=params(max(held + (8 << 20), 56 << 20)),
        cost_estimate=cost(rows * NUW * BLOCK * table * BLOCK * OCC, tiles.size * 2 + coeff.size * 2),
        name="first_section",
    )(aux, ao, owner, tiles, coeff)


def later_kernel(left, coeff, keep, send):
    pairs, _, span = keep.shape
    for part, out in ((1, send), (0, keep)):
        for p in range(0, pairs, 2):
            at = part * pairs + p
            value = jnp.dot(
                left[at : at + 2].reshape(2 * BLOCK, left.shape[2]), coeff[...], preferred_element_type=jnp.float32
            )
            out[p : p + 2] = value.astype(jnp.bfloat16).reshape(2, BLOCK, span)


def later_section(left, coeff):
    rows = left.shape[0]
    half = jax.ShapeDtypeStruct((rows // 2, BLOCK, OCC), jnp.bfloat16)
    return pl.pallas_call(
        later_kernel,
        in_specs=[vmem(), vmem()],
        out_specs=[vmem(), vmem()],
        out_shape=[half, half],
        compiler_params=params(2 * SMALL_VMEM),
        cost_estimate=cost(left.size * 2 * OCC, left.size * 4),
        name="later_section",
    )(left, coeff)


def metric_kernel(ys, plan, slots, outs_of, metric, keep, send, dense):
    col = lax.axis_index("col")
    y, core = col // 2, col % 2

    @pl.loop(0, dense.shape[0])
    def _(k):
        dense[k] = jnp.zeros((BLOCK, BLOCK), jnp.float32)

    @pl.loop(0, metric.shape[0])
    def _(k):
        where = outs_of[k] * 4 + plan[2 + slots[k]]
        dense[where] += metric[k].astype(jnp.float32)

    for target, mine in ((keep, core), (send, 1 - core)):
        for d in range(ys):
            to_col = lax.rem(y + d, ys) * 2 + mine
            for h in range(QB_DEV):
                for spot in range(3):
                    target[d, h * BLOCK : (h + 1) * BLOCK, spot * BLOCK : (spot + 1) * BLOCK] = dense[
                        (to_col * QB_DEV + h) * 4 + spot
                    ].astype(jnp.bfloat16)


def metric_section(plan, slots, outs_of, metric, cols):
    ys = cols // 2
    shape = jax.ShapeDtypeStruct((ys, QB_DEV * BLOCK, 3 * BLOCK), jnp.bfloat16)
    return pl.pallas_call(
        functools.partial(metric_kernel, ys),
        in_specs=[smem(), smem(), smem(), vmem()],
        out_specs=[vmem(), vmem()],
        out_shape=[shape, shape],
        scratch_shapes=[pltpu.VMEM((cols * QB_DEV * 4, BLOCK, BLOCK), jnp.float32)],
        compiler_params=params(2 * SMALL_VMEM),
        cost_estimate=cost(0, metric.size * 2 + cols * 400000),
        name="metric_section",
    )(plan, slots, outs_of, metric)


def middle_kernel(pairs, plan, mine, other, own, outward):
    def total(k):
        return (mine[k].astype(jnp.float32) + other[k].astype(jnp.float32)).astype(jnp.bfloat16)

    shift = jnp.where(lax.axis_index("row") // 2 < pairs // 2, 0, 2)
    base = plan[0]
    for k in range(2):
        own[k] = total(base + k)
    for k in range(pairs - 2):
        outward[k] = total(shift + k)


def middle_section(plan, mine, other):
    pairs, _, span = mine.shape
    return pl.pallas_call(
        functools.partial(middle_kernel, pairs),
        in_specs=[smem(), vmem(), vmem()],
        out_specs=[vmem(), vmem()],
        out_shape=[
            jax.ShapeDtypeStruct((2, BLOCK, span), jnp.bfloat16),
            jax.ShapeDtypeStruct((pairs - 2, BLOCK, span), jnp.bfloat16),
        ],
        compiler_params=params(),
        cost_estimate=cost(mine.size, mine.size * 6),
        name="middle_section",
    )(plan, mine, other)


def outward_kernel(pairs, level, plan, own, came, own_out, rest):
    z = lax.axis_index("row") // 2
    lower = z < pairs // 2
    distance = jnp.where(lower, pairs // 2 - 1 - z, z - pairs // 2)
    here = distance == level
    base = plan[0]

    @pl.when(here)
    def _():
        for k in range(2):
            own_out[k] = came[base + k]

    @pl.when(jnp.logical_not(here))
    def _():
        for k in range(2):
            own_out[k] = own[k]

    if level == pairs // 2 - 1:
        rest[0] = own_out[plan[1]]
    else:
        shift = jnp.where(lower, 0, 2)
        for k in range(rest.shape[0]):
            rest[k] = came[shift + k]


def outward_section(plan, own, came, level, pairs):
    span = own.shape[2]
    last = level == pairs // 2 - 1
    return pl.pallas_call(
        functools.partial(outward_kernel, pairs, level),
        in_specs=[smem(), vmem(), vmem()],
        out_specs=[vmem(), vmem()],
        out_shape=[
            jax.ShapeDtypeStruct((2, BLOCK, span), jnp.bfloat16),
            jax.ShapeDtypeStruct((1 if last else came.shape[0] - 2, BLOCK, span), jnp.bfloat16),
        ],
        compiler_params=params(),
        cost_estimate=cost(0, own.size * 8),
        name="outward_section",
    )(plan, own, came)


def term_kernel(ys, keep, got, own, own_core, fix, fix_core, sent, kept):
    span = own.shape[2]
    right = jnp.concatenate(
        [
            own[...].reshape(2 * BLOCK, span),
            fix[0],
            own_core[...].reshape(2 * BLOCK, span),
            fix_core[0],
        ],
        axis=0,
    )
    for d in range(ys - 1, -1, -1):
        left = jnp.concatenate([keep[d], got[d]], axis=1)
        made = jnp.dot(left, right, preferred_element_type=jnp.float32)
        if d:
            sent[d - 1] = made.astype(jnp.bfloat16)
        else:
            kept[...] = made


def term_section(keep, got, own, own_core, fix, fix_core):
    ys = keep.shape[0]
    span = own.shape[2]
    return pl.pallas_call(
        functools.partial(term_kernel, ys),
        in_specs=[vmem()] * 6,
        out_specs=[vmem(), vmem()],
        out_shape=[
            jax.ShapeDtypeStruct((ys - 1, QB_DEV * BLOCK, span), jnp.bfloat16),
            jax.ShapeDtypeStruct((QB_DEV * BLOCK, span), jnp.float32),
        ],
        compiler_params=params(),
        cost_estimate=cost(2 * ys * QB_DEV * BLOCK * 6 * BLOCK * span, keep.size * 4 + span * BLOCK * 24),
        name="term_section",
    )(keep, got, own, own_core, fix, fix_core)


def added(a, b):
    return (a.astype(jnp.float32) + b.astype(jnp.float32)).astype(jnp.bfloat16)


def per_device(
    coeff, tri_blocks, pair_aux, pair_ao, owner_slot, metric_blocks, pair_slot, pair_out
):
    rows = lax.axis_size("row")
    cols = lax.axis_size("col")
    pairs, ys = rows // 2, cols // 2
    half = pairs // 2

    def on_line(moves):
        return [(2 * a + x, 2 * b + x) for a, b in moves for x in range(2)]

    swap_pair = [(r, r ^ 1) for r in range(rows)]
    swap_core = [(c, c ^ 1) for c in range(cols)]

    *early, plan, left = first_section(tri_blocks, pair_aux, pair_ao, owner_slot, coeff, rows)
    made = (*early, *later_section(left, coeff))
    keep, send = metric_section(plan, pair_slot, pair_out, metric_blocks, cols)
    got = lax.ppermute(send, "col", swap_core)

    finished = []
    for piece in range(NUW):
        total = added(made[2 * piece], lax.ppermute(made[2 * piece + 1], "row", swap_pair))
        for a in range(half - 1):
            inward = on_line([(a, a + 1), (pairs - 1 - a, pairs - 2 - a)])
            total = added(total, lax.ppermute(total, "row", inward))
        other = lax.ppermute(total, "row", on_line([(half - 1, half), (half, half - 1)]))
        own, rest = middle_section(plan, total, other)
        for level in range(1, half):
            outward = on_line([(half - level, half - 1 - level), (half - 1 + level, half + level)])
            own, rest = outward_section(plan, own, lax.ppermute(rest, "row", outward), level, pairs)
        fix = lax.ppermute(rest, "row", swap_pair)
        own_core = lax.ppermute(own, "col", swap_core)
        fix_core = lax.ppermute(fix, "col", swap_core)
        sent, kept = term_section(keep, got, own, own_core, fix, fix_core)
        for d in range(1, ys):
            around = [(2 * y + k, 2 * ((y + d) % ys) + k) for y in range(ys) for k in range(2)]
            kept = kept + lax.ppermute(sent[d - 1], "col", around).astype(jnp.float32)
        finished.append(kept.astype(jnp.bfloat16))
    return jnp.concatenate(finished, axis=1)


def solution(mesh):
    in_specs = (
        P("row", None),
        P(("row", "col"), None, None),
        P(("row", "col")),
        P(("row", "col")),
        P("col", None),
        P(("row", "col"), None, None),
        P(("row", "col")),
        P(("row", "col")),
    )
    out_specs = P(("row", "col"), None)
    return jax.shard_map(
        per_device, mesh=mesh, in_specs=in_specs, out_specs=out_specs, check_vma=False
    )
```

```python
import functools
import math

import jax
import jax.numpy as jnp
from jax import lax
from jax.experimental import pallas as pl
from jax.experimental.pallas import tpu as pltpu
from jax.sharding import PartitionSpec as P

BLOCK = 128
OCC = 512
NUW = 2
MAXOWN = 2
QB_DEV = 2
SMALL_VMEM = 8 << 20


def smem():
    return pl.BlockSpec(memory_space=pltpu.SMEM)


def vmem():
    return pl.BlockSpec(memory_space=pltpu.VMEM)


def params(limit=SMALL_VMEM):
    return pltpu.CompilerParams(vmem_limit_bytes=limit)


def cost(flops, moved):
    return pl.CostEstimate(flops=int(flops), bytes_accessed=int(moved), transcendentals=0)


def write_plan(rows, owner, plan, occ, order, place, moved_flag, start):
    pairs = rows // 2
    i32 = jnp.int32
    for s in range(2 * rows):
        occ[s] = i32(-1)
    for j in range(rows):
        occ[owner[0, j]] = i32(j)
    held = [occ[s] for s in range(2 * rows)]
    has = [(h >= 0).astype(i32) for h in held]
    first_side = sum(has[4 * z] + has[4 * z + 1] for z in range(pairs))
    giver = jnp.where(first_side > pairs, i32(0), i32(1))
    need = jnp.abs(first_side - pairs)
    moved = i32(0)
    counts = [i32(0), i32(0)]
    for z in range(pairs):
        n0 = has[4 * z] + has[4 * z + 1]
        n1 = has[4 * z + 2] + has[4 * z + 3]
        from_count = jnp.where(giver == 0, n0, n1)
        to_count = n0 + n1 - from_count
        move = jnp.logical_and(moved < need, jnp.logical_and(from_count >= 1, to_count <= 1)).astype(i32)
        moved = moved + move
        start[z] = counts[0]
        start[pairs + z] = counts[1]
        for x in range(2):
            for parity in range(2):
                s = 4 * z + 2 * x + parity
                pick = has[s] if parity else has[s] * (1 - has[s + 1])
                chosen = move * pick * jnp.where(giver == x, i32(1), i32(0))
                side = jnp.where(chosen == 1, i32(1 - x), i32(x))
                spot = jnp.where(side == 0, counts[0], counts[1])
                order[jnp.where(has[s] == 1, side * pairs + spot, i32(2 * pairs))] = held[s]
                place[s] = jnp.where(has[s] == 1, spot, i32(-1))
                moved_flag[s] = chosen
                counts[0] = counts[0] + has[s] * (1 - side)
                counts[1] = counts[1] + has[s] * side
    row = lax.axis_index("row")
    z, x = row // 2, row % 2
    base = jnp.minimum(start[x * pairs + z], pairs - 2)
    away = i32(0)
    for parity in range(2):
        s = 4 * z + 2 * (1 - x) + parity
        away = jnp.where(moved_flag[s] == 1, place[s] - base, away)
    plan[0] = away
    for parity in range(2):
        s = 2 * row + parity
        where = jnp.where(moved_flag[s] == 1, i32(2), place[s] - base)
        plan[1 + parity] = jnp.where(place[s] >= 0, where, i32(3))
    plan[3] = base


def first_kernel(
    rows, table, group, aux_in, ao_in, owner_in, tiles_in, coeff_in, keep, send, plan, later,
    tiles, coeff, dense, made, left_later, aux, ao, owner, occ, order, place, moved_flag, start, sems, out_sems,
):
    pairs = rows // 2
    groups = tiles.shape[0]
    small = [
        pltpu.make_async_copy(aux_in, aux, sems.at[groups]),
        pltpu.make_async_copy(ao_in, ao, sems.at[groups + 1]),
        pltpu.make_async_copy(owner_in, owner, sems.at[groups + 2]),
    ]
    loads = [
        pltpu.make_async_copy(tiles_in.at[pl.ds(g * group, group)], tiles.at[g], sems.at[g]) for g in range(groups)
    ]
    table_load = pltpu.make_async_copy(coeff_in, coeff, sems.at[groups + 3])
    for copy in (*small, *loads, table_load):
        copy.start()

    @pl.loop(0, rows * table, unroll=4)
    def _(k):
        dense[k] = jnp.zeros((NUW * BLOCK, BLOCK), jnp.float32)

    for copy in small:
        copy.wait()
    write_plan(rows, owner, plan, occ, order, place, moved_flag, start)

    for g in range(groups):
        loads[g].wait()

        @pl.loop(0, group, unroll=4)
        def _(t):
            k = g * group + t
            where = aux[k] * table + ao[k]
            dense[where] += tiles[g, t].astype(jnp.float32)

    table_load.wait()
    x = lax.axis_index("row") % 2
    stores = []
    for part, out in ((1, send), (0, keep)):
        side = x if part == 0 else 1 - x
        for p in range(pairs // 2):
            at = part * pairs + 2 * p
            for nu in range(NUW):
                blocks = []
                for h in range(2):
                    j = order[side * pairs + 2 * p + h]
                    blocks.append(
                        jnp.concatenate(
                            [
                                dense[j * table + a, pl.ds(nu, BLOCK, stride=NUW), :].astype(jnp.bfloat16)
                                for a in range(table)
                            ],
                            axis=1,
                        )
                    )
                left = jnp.concatenate(blocks, axis=0)
                if nu:
                    left_later[at : at + 2] = left.reshape(2, BLOCK, table * BLOCK)
                    stores.append((left_later.at[pl.ds(at, 2)], later.at[pl.ds(at, 2)]))
                else:
                    value = jnp.dot(left, coeff[...], preferred_element_type=jnp.float32)
                    made[at : at + 2] = value.astype(jnp.bfloat16).reshape(2, BLOCK, OCC)
                    stores.append((made.at[pl.ds(at, 2)], out.at[pl.ds(2 * p, 2)]))
                stores[-1] = pltpu.make_async_copy(*stores[-1], out_sems.at[len(stores) - 1])
                stores[-1].start()
    for copy in stores:
        copy.wait()


def first_section(tiles, aux, ao, owner, coeff, rows):
    count = tiles.shape[0]
    table = coeff.shape[0] // BLOCK
    group = math.gcd(count, 20)
    groups = count // group
    pairs = rows // 2
    any_space = pl.BlockSpec(memory_space=pl.ANY)
    half = jax.ShapeDtypeStruct((pairs, BLOCK, OCC), jnp.bfloat16)
    held = 2 * tiles.size + 2 * coeff.size + rows * table * NUW * BLOCK * BLOCK * 4 + rows * BLOCK * 4 * OCC * 2
    return pl.pallas_call(
        functools.partial(first_kernel, rows, table, group),
        in_specs=[any_space] * 5,
        out_specs=[any_space, any_space, smem(), any_space],
        out_shape=[
            half,
            half,
            jax.ShapeDtypeStruct((4,), jnp.int32),
            jax.ShapeDtypeStruct((rows, BLOCK, table * BLOCK), jnp.bfloat16),
        ],
        scratch_shapes=[
            pltpu.VMEM((groups, group, NUW * BLOCK, BLOCK), jnp.bfloat16),
            pltpu.VMEM(coeff.shape, jnp.bfloat16),
            pltpu.VMEM((rows * table, NUW * BLOCK, BLOCK), jnp.float32),
            pltpu.VMEM((rows, BLOCK, OCC), jnp.bfloat16),
            pltpu.VMEM((rows, BLOCK, table * BLOCK), jnp.bfloat16),
            pltpu.SMEM((count,), jnp.int32),
            pltpu.SMEM((count,), jnp.int32),
            pltpu.SMEM(owner.shape, jnp.int32),
            pltpu.SMEM((2 * rows,), jnp.int32),
            pltpu.SMEM((2 * pairs + 1,), jnp.int32),
            pltpu.SMEM((2 * rows,), jnp.int32),
            pltpu.SMEM((2 * rows,), jnp.int32),
            pltpu.SMEM((2 * pairs,), jnp.int32),
            pltpu.SemaphoreType.DMA((groups + 4,)),
            pltpu.SemaphoreType.DMA((NUW * pairs,)),
        ],
        compiler_params=params(max(held + (8 << 20), 56 << 20)),
        cost_estimate=cost(rows * NUW * BLOCK * table * BLOCK * OCC, tiles.size * 2 + coeff.size * 2),
        name="first_section",
    )(aux, ao, owner, tiles, coeff)


def later_kernel(left, coeff, keep, send):
    pairs, _, span = keep.shape
    for part, out in ((1, send), (0, keep)):
        for p in range(0, pairs, 2):
            at = part * pairs + p
            value = jnp.dot(
                left[at : at + 2].reshape(2 * BLOCK, left.shape[2]), coeff[...], preferred_element_type=jnp.float32
            )
            out[p : p + 2] = value.astype(jnp.bfloat16).reshape(2, BLOCK, span)


def later_section(left, coeff):
    rows = left.shape[0]
    half = jax.ShapeDtypeStruct((rows // 2, BLOCK, OCC), jnp.bfloat16)
    return pl.pallas_call(
        later_kernel,
        in_specs=[vmem(), vmem()],
        out_specs=[vmem(), vmem()],
        out_shape=[half, half],
        compiler_params=params(2 * SMALL_VMEM),
        cost_estimate=cost(left.size * 2 * OCC, left.size * 4),
        name="later_section",
    )(left, coeff)


def metric_kernel(ys, plan, slots, outs_of, metric, keep, send, dense):
    col = lax.axis_index("col")
    y, core = col // 2, col % 2

    @pl.loop(0, dense.shape[0])
    def _(k):
        dense[k] = jnp.zeros((BLOCK, BLOCK), jnp.float32)

    @pl.loop(0, metric.shape[0])
    def _(k):
        where = outs_of[k] * 4 + plan[1 + slots[k]]
        dense[where] += metric[k].astype(jnp.float32)

    for target, mine in ((keep, core), (send, 1 - core)):
        for d in range(ys):
            to_col = lax.rem(y + d, ys) * 2 + mine
            for h in range(QB_DEV):
                for spot in range(3):
                    target[d, h * BLOCK : (h + 1) * BLOCK, spot * BLOCK : (spot + 1) * BLOCK] = dense[
                        (to_col * QB_DEV + h) * 4 + spot
                    ].astype(jnp.bfloat16)


def metric_section(plan, slots, outs_of, metric, cols):
    ys = cols // 2
    shape = jax.ShapeDtypeStruct((ys, QB_DEV * BLOCK, 3 * BLOCK), jnp.bfloat16)
    return pl.pallas_call(
        functools.partial(metric_kernel, ys),
        in_specs=[smem(), smem(), smem(), vmem()],
        out_specs=[vmem(), vmem()],
        out_shape=[shape, shape],
        scratch_shapes=[pltpu.VMEM((cols * QB_DEV * 4, BLOCK, BLOCK), jnp.float32)],
        compiler_params=params(2 * SMALL_VMEM),
        cost_estimate=cost(0, metric.size * 2 + cols * 400000),
        name="metric_section",
    )(plan, slots, outs_of, metric)


def pair_kernel(mine, came, near, far):
    half = near.shape[0]
    upper = (lax.axis_index("row") // 2 >= half).astype(jnp.int32)
    for out, first in ((near, upper * half), (far, (1 - upper) * half)):
        for k in range(half):
            total = mine[first + k].astype(jnp.float32) + came[first + k].astype(jnp.float32)
            out[k] = total.astype(jnp.bfloat16)


def pair_section(mine, came):
    pairs, _, span = mine.shape
    return pl.pallas_call(
        pair_kernel,
        in_specs=[vmem(), vmem()],
        out_specs=[vmem()] * 2,
        out_shape=[jax.ShapeDtypeStruct((pairs // 2, BLOCK, span), jnp.bfloat16)] * 2,
        compiler_params=params(),
        cost_estimate=cost(mine.size, mine.size * 6),
        name="pair_section",
    )(mine, came)


def line_kernel(*refs):
    *parts, out = refs
    for k in range(out.shape[0]):
        total = parts[0][k].astype(jnp.float32)
        for part in parts[1:]:
            total = total + part[k].astype(jnp.float32)
        out[k] = total.astype(jnp.bfloat16)


def line_section(parts):
    return pl.pallas_call(
        line_kernel,
        in_specs=[vmem()] * len(parts),
        out_specs=vmem(),
        out_shape=jax.ShapeDtypeStruct(parts[0].shape, jnp.bfloat16),
        compiler_params=params(),
        cost_estimate=cost(parts[0].size * len(parts), parts[0].size * 2 * len(parts)),
        name="line_section",
    )(*parts)


def owned_kernel(half, plan, *refs):
    *held, owned, away = refs
    z = lax.axis_index("row") // 2
    upper = (z >= half).astype(jnp.int32)
    distance = jnp.where(z >= half, z - half, half - 1 - z)
    for k in range(2):
        block = plan[3] + k
        block_upper = (block >= half).astype(jnp.int32)
        wanted = distance + half * jnp.abs(block_upper - upper)
        for d, blocks in enumerate(held):

            @pl.when(wanted == d)
            def _(blocks=blocks):
                owned[k] = blocks[block - half * block_upper]

    away[0] = owned[plan[0]]


def owned_section(plan, held):
    half, _, span = held[0].shape
    return pl.pallas_call(
        functools.partial(owned_kernel, half),
        in_specs=[smem()] + [vmem()] * len(held),
        out_specs=[vmem(), vmem()],
        out_shape=[
            jax.ShapeDtypeStruct((2, BLOCK, span), jnp.bfloat16),
            jax.ShapeDtypeStruct((1, BLOCK, span), jnp.bfloat16),
        ],
        compiler_params=params(),
        cost_estimate=cost(0, held[0].size * 12),
        name="owned_section",
    )(plan, *held)


def term_kernel(ys, keep, got, own, own_core, fix, fix_core, sent, kept):
    span = own.shape[2]
    right = jnp.concatenate(
        [
            own[...].reshape(2 * BLOCK, span),
            fix[0],
            own_core[...].reshape(2 * BLOCK, span),
            fix_core[0],
        ],
        axis=0,
    )
    for d in range(ys - 1, -1, -1):
        left = jnp.concatenate([keep[d], got[d]], axis=1)
        made = jnp.dot(left, right, preferred_element_type=jnp.float32)
        if d:
            sent[d - 1] = made.astype(jnp.bfloat16)
        else:
            kept[...] = made


def term_section(keep, got, own, own_core, fix, fix_core):
    ys = keep.shape[0]
    span = own.shape[2]
    return pl.pallas_call(
        functools.partial(term_kernel, ys),
        in_specs=[vmem()] * 6,
        out_specs=[vmem(), vmem()],
        out_shape=[
            jax.ShapeDtypeStruct((ys - 1, QB_DEV * BLOCK, span), jnp.bfloat16),
            jax.ShapeDtypeStruct((QB_DEV * BLOCK, span), jnp.float32),
        ],
        compiler_params=params(),
        cost_estimate=cost(2 * ys * QB_DEV * BLOCK * 6 * BLOCK * span, keep.size * 4 + span * BLOCK * 24),
        name="term_section",
    )(keep, got, own, own_core, fix, fix_core)


def per_device(
    coeff, tri_blocks, pair_aux, pair_ao, owner_slot, metric_blocks, pair_slot, pair_out
):
    rows = lax.axis_size("row")
    cols = lax.axis_size("col")
    pairs, ys = rows // 2, cols // 2

    def on_line(moves):
        return [(2 * a + x, 2 * b + x) for a, b in moves for x in range(2)]

    swap_pair = [(r, r ^ 1) for r in range(rows)]
    swap_core = [(c, c ^ 1) for c in range(cols)]

    *early, plan, left = first_section(tri_blocks, pair_aux, pair_ao, owner_slot, coeff, rows)
    made = (*early, *later_section(left, coeff))
    keep, send = metric_section(plan, pair_slot, pair_out, metric_blocks, cols)
    got = lax.ppermute(send, "col", swap_core)

    half = pairs // 2
    near_moves = [[(half - 1 - e, half - 1), (half + e, half)] for e in range(1, half)]
    far_moves = [[(half - 1 - e, half), (half + e, half - 1)] for e in range(half)]
    inward = [on_line(m) for m in near_moves], [on_line(m) for m in far_moves]
    beyond = pairs - (pairs - half) // 2 - half
    outward = [on_line([(b, a) for a, b in m]) for m in near_moves] + [
        on_line([(half - 1, half + e), (half, half - 1 - e)]) for e in range(beyond)
    ]
    around = [
        [(2 * y + k, 2 * ((y + d) % ys) + k) for y in range(ys) for k in range(2)] for d in range(1, ys)
    ]

    finished = []
    for piece in range(NUW):
        came = lax.ppermute(made[2 * piece + 1], "row", swap_pair)
        near, far = pair_section(made[2 * piece], came)
        parts = [lax.ppermute(far, "row", moves) for moves in inward[1]]
        parts += [lax.ppermute(near, "row", moves) for moves in inward[0]]
        host = line_section([near, *parts])
        held = [host] + [lax.ppermute(host, "row", moves) for moves in outward]
        own, away = owned_section(plan, held)
        fix = lax.ppermute(away, "row", swap_pair)
        own_core = lax.ppermute(own, "col", swap_core)
        fix_core = lax.ppermute(fix, "col", swap_core)
        sent, kept = term_section(keep, got, own, own_core, fix, fix_core)
        for d in range(1, ys):
            kept = kept + lax.ppermute(sent[d - 1], "col", around[d - 1]).astype(jnp.float32)
        finished.append(kept.astype(jnp.bfloat16))
    return jnp.concatenate(finished, axis=1)


def solution(mesh):
    in_specs = (
        P("row", None),
        P(("row", "col"), None, None),
        P(("row", "col")),
        P(("row", "col")),
        P("col", None),
        P(("row", "col"), None, None),
        P(("row", "col")),
        P(("row", "col")),
    )
    out_specs = P(("row", "col"), None)
    return jax.shard_map(
        per_device, mesh=mesh, in_specs=in_specs, out_specs=out_specs, check_vma=False
    )
```

```python
import functools
import math

import jax
import jax.numpy as jnp
from jax import lax
from jax.experimental import pallas as pl
from jax.experimental.pallas import tpu as pltpu
from jax.sharding import PartitionSpec as P

BLOCK = 128
OCC = 512
NUW = 2
MAXOWN = 2
QB_DEV = 2
SMALL_VMEM = 8 << 20


def smem():
    return pl.BlockSpec(memory_space=pltpu.SMEM)


def vmem():
    return pl.BlockSpec(memory_space=pltpu.VMEM)


def params(limit=SMALL_VMEM):
    return pltpu.CompilerParams(vmem_limit_bytes=limit)


def cost(flops, moved):
    return pl.CostEstimate(flops=int(flops), bytes_accessed=int(moved), transcendentals=0)


def write_plan(rows, owner, plan, occ, order, place, moved_flag, start):
    pairs = rows // 2
    i32 = jnp.int32
    for s in range(2 * rows):
        occ[s] = i32(-1)
    for j in range(rows):
        occ[owner[0, j]] = i32(j)
    held = [occ[s] for s in range(2 * rows)]
    has = [(h >= 0).astype(i32) for h in held]
    first_side = sum(has[4 * z] + has[4 * z + 1] for z in range(pairs))
    giver = jnp.where(first_side > pairs, i32(0), i32(1))
    need = jnp.abs(first_side - pairs)
    moved = i32(0)
    counts = [i32(0), i32(0)]
    for z in range(pairs):
        n0 = has[4 * z] + has[4 * z + 1]
        n1 = has[4 * z + 2] + has[4 * z + 3]
        from_count = jnp.where(giver == 0, n0, n1)
        to_count = n0 + n1 - from_count
        move = jnp.logical_and(moved < need, jnp.logical_and(from_count >= 1, to_count <= 1)).astype(i32)
        moved = moved + move
        start[z] = counts[0]
        start[pairs + z] = counts[1]
        for x in range(2):
            for parity in range(2):
                s = 4 * z + 2 * x + parity
                pick = has[s] if parity else has[s] * (1 - has[s + 1])
                chosen = move * pick * jnp.where(giver == x, i32(1), i32(0))
                side = jnp.where(chosen == 1, i32(1 - x), i32(x))
                spot = jnp.where(side == 0, counts[0], counts[1])
                order[jnp.where(has[s] == 1, side * pairs + spot, i32(2 * pairs))] = held[s]
                place[s] = jnp.where(has[s] == 1, spot, i32(-1))
                moved_flag[s] = chosen
                counts[0] = counts[0] + has[s] * (1 - side)
                counts[1] = counts[1] + has[s] * side
    row = lax.axis_index("row")
    z, x = row // 2, row % 2
    base = jnp.minimum(start[x * pairs + z], pairs - 2)
    away = i32(0)
    for parity in range(2):
        s = 4 * z + 2 * (1 - x) + parity
        away = jnp.where(moved_flag[s] == 1, place[s] - base, away)
    plan[0] = away
    for parity in range(2):
        s = 2 * row + parity
        where = jnp.where(moved_flag[s] == 1, i32(2), place[s] - base)
        plan[1 + parity] = jnp.where(place[s] >= 0, where, i32(3))
    plan[3] = base


def first_kernel(
    rows, table, group, aux_in, ao_in, owner_in, tiles_in, coeff_in, keep, send, plan, later,
    tiles, coeff, dense, made, left_later, aux, ao, owner, occ, order, place, moved_flag, start, sems, out_sems,
):
    pairs = rows // 2
    groups = tiles.shape[0]
    small = [
        pltpu.make_async_copy(aux_in, aux, sems.at[groups]),
        pltpu.make_async_copy(ao_in, ao, sems.at[groups + 1]),
        pltpu.make_async_copy(owner_in, owner, sems.at[groups + 2]),
    ]
    loads = [
        pltpu.make_async_copy(tiles_in.at[pl.ds(g * group, group)], tiles.at[g], sems.at[g]) for g in range(groups)
    ]
    table_load = pltpu.make_async_copy(coeff_in, coeff, sems.at[groups + 3])
    for copy in (*small, *loads, table_load):
        copy.start()

    @pl.loop(0, rows * table, unroll=4)
    def _(k):
        dense[k] = jnp.zeros((NUW * BLOCK, BLOCK), jnp.float32)

    for copy in small:
        copy.wait()
    write_plan(rows, owner, plan, occ, order, place, moved_flag, start)

    for g in range(groups):
        loads[g].wait()

        @pl.loop(0, group, unroll=4)
        def _(t):
            k = g * group + t
            where = aux[k] * table + ao[k]
            dense[where] += tiles[g, t].astype(jnp.float32)

    table_load.wait()
    x = lax.axis_index("row") % 2
    stores = []
    for part, out in ((1, send), (0, keep)):
        side = x if part == 0 else 1 - x
        for p in range(pairs // 2):
            at = part * pairs + 2 * p
            for nu in range(NUW):
                blocks = []
                for h in range(2):
                    j = order[side * pairs + 2 * p + h]
                    blocks.append(
                        jnp.concatenate(
                            [
                                dense[j * table + a, pl.ds(nu, BLOCK, stride=NUW), :].astype(jnp.bfloat16)
                                for a in range(table)
                            ],
                            axis=1,
                        )
                    )
                left = jnp.concatenate(blocks, axis=0)
                if nu:
                    left_later[at : at + 2] = left.reshape(2, BLOCK, table * BLOCK)
                    stores.append((left_later.at[pl.ds(at, 2)], later.at[pl.ds(at, 2)]))
                else:
                    value = jnp.dot(left, coeff[...], preferred_element_type=jnp.float32)
                    made[at : at + 2] = value.astype(jnp.bfloat16).reshape(2, BLOCK, OCC)
                    stores.append((made.at[pl.ds(at, 2)], out.at[pl.ds(2 * p, 2)]))
                stores[-1] = pltpu.make_async_copy(*stores[-1], out_sems.at[len(stores) - 1])
                stores[-1].start()
    for copy in stores:
        copy.wait()


def first_section(tiles, aux, ao, owner, coeff, rows):
    count = tiles.shape[0]
    table = coeff.shape[0] // BLOCK
    group = math.gcd(count, 20)
    groups = count // group
    pairs = rows // 2
    any_space = pl.BlockSpec(memory_space=pl.ANY)
    half = jax.ShapeDtypeStruct((pairs, BLOCK, OCC), jnp.bfloat16)
    held = 2 * tiles.size + 2 * coeff.size + rows * table * NUW * BLOCK * BLOCK * 4 + rows * BLOCK * 4 * OCC * 2
    return pl.pallas_call(
        functools.partial(first_kernel, rows, table, group),
        in_specs=[any_space] * 5,
        out_specs=[any_space, any_space, smem(), any_space],
        out_shape=[
            half,
            half,
            jax.ShapeDtypeStruct((4,), jnp.int32),
            jax.ShapeDtypeStruct((rows, BLOCK, table * BLOCK), jnp.bfloat16),
        ],
        scratch_shapes=[
            pltpu.VMEM((groups, group, NUW * BLOCK, BLOCK), jnp.bfloat16),
            pltpu.VMEM(coeff.shape, jnp.bfloat16),
            pltpu.VMEM((rows * table, NUW * BLOCK, BLOCK), jnp.float32),
            pltpu.VMEM((rows, BLOCK, OCC), jnp.bfloat16),
            pltpu.VMEM((rows, BLOCK, table * BLOCK), jnp.bfloat16),
            pltpu.SMEM((count,), jnp.int32),
            pltpu.SMEM((count,), jnp.int32),
            pltpu.SMEM(owner.shape, jnp.int32),
            pltpu.SMEM((2 * rows,), jnp.int32),
            pltpu.SMEM((2 * pairs + 1,), jnp.int32),
            pltpu.SMEM((2 * rows,), jnp.int32),
            pltpu.SMEM((2 * rows,), jnp.int32),
            pltpu.SMEM((2 * pairs,), jnp.int32),
            pltpu.SemaphoreType.DMA((groups + 4,)),
            pltpu.SemaphoreType.DMA((NUW * pairs,)),
        ],
        compiler_params=params(max(held + (8 << 20), 56 << 20)),
        cost_estimate=cost(rows * NUW * BLOCK * table * BLOCK * OCC, tiles.size * 2 + coeff.size * 2),
        name="first_section",
    )(aux, ao, owner, tiles, coeff)


def later_kernel(left, coeff, keep, send):
    pairs, _, span = keep.shape
    for part, out in ((1, send), (0, keep)):
        for p in range(0, pairs, 2):
            at = part * pairs + p
            value = jnp.dot(
                left[at : at + 2].reshape(2 * BLOCK, left.shape[2]), coeff[...], preferred_element_type=jnp.float32
            )
            out[p : p + 2] = value.astype(jnp.bfloat16).reshape(2, BLOCK, span)


def later_section(left, coeff):
    rows = left.shape[0]
    half = jax.ShapeDtypeStruct((rows // 2, BLOCK, OCC), jnp.bfloat16)
    return pl.pallas_call(
        later_kernel,
        in_specs=[vmem(), vmem()],
        out_specs=[vmem(), vmem()],
        out_shape=[half, half],
        compiler_params=params(2 * SMALL_VMEM),
        cost_estimate=cost(left.size * 2 * OCC, left.size * 4),
        name="later_section",
    )(left, coeff)


def metric_kernel(ys, plan, slots, outs_of, metric, keep, send, dense):
    col = lax.axis_index("col")
    y, core = col // 2, col % 2

    @pl.loop(0, dense.shape[0])
    def _(k):
        dense[k] = jnp.zeros((BLOCK, BLOCK), jnp.float32)

    @pl.loop(0, metric.shape[0])
    def _(k):
        where = outs_of[k] * 4 + plan[1 + slots[k]]
        dense[where] += metric[k].astype(jnp.float32)

    for target, mine in ((keep, core), (send, 1 - core)):
        for d in range(ys):
            to_col = lax.rem(y + d, ys) * 2 + mine
            for h in range(QB_DEV):
                for spot in range(3):
                    target[d, h * BLOCK : (h + 1) * BLOCK, spot * BLOCK : (spot + 1) * BLOCK] = dense[
                        (to_col * QB_DEV + h) * 4 + spot
                    ].astype(jnp.bfloat16)


def metric_section(plan, slots, outs_of, metric, cols):
    ys = cols // 2
    shape = jax.ShapeDtypeStruct((ys, QB_DEV * BLOCK, 3 * BLOCK), jnp.bfloat16)
    return pl.pallas_call(
        functools.partial(metric_kernel, ys),
        in_specs=[smem(), smem(), smem(), vmem()],
        out_specs=[vmem(), vmem()],
        out_shape=[shape, shape],
        scratch_shapes=[pltpu.VMEM((cols * QB_DEV * 4, BLOCK, BLOCK), jnp.float32)],
        compiler_params=params(2 * SMALL_VMEM),
        cost_estimate=cost(0, metric.size * 2 + cols * 400000),
        name="metric_section",
    )(plan, slots, outs_of, metric)


def pair_kernel(mine, came, near, far):
    half = near.shape[0]
    upper = (lax.axis_index("row") // 2 >= half).astype(jnp.int32)
    for out, first in ((near, upper * half), (far, (1 - upper) * half)):
        for k in range(half):
            total = mine[first + k].astype(jnp.float32) + came[first + k].astype(jnp.float32)
            out[k] = total.astype(jnp.bfloat16)


def pair_section(mine, came):
    pairs, _, span = mine.shape
    return pl.pallas_call(
        pair_kernel,
        in_specs=[vmem(), vmem()],
        out_specs=[vmem()] * 2,
        out_shape=[jax.ShapeDtypeStruct((pairs // 2, BLOCK, span), jnp.bfloat16)] * 2,
        compiler_params=params(),
        cost_estimate=cost(mine.size, mine.size * 6),
        name="pair_section",
    )(mine, came)


def line_kernel(*refs):
    *parts, out = refs
    for k in range(out.shape[0]):
        total = parts[0][k].astype(jnp.float32)
        for part in parts[1:]:
            total = total + part[k].astype(jnp.float32)
        out[k] = total.astype(jnp.bfloat16)


def line_section(parts):
    return pl.pallas_call(
        line_kernel,
        in_specs=[vmem()] * len(parts),
        out_specs=vmem(),
        out_shape=jax.ShapeDtypeStruct(parts[0].shape, jnp.bfloat16),
        compiler_params=params(),
        cost_estimate=cost(parts[0].size * len(parts), parts[0].size * 2 * len(parts)),
        name="line_section",
    )(*parts)


def owned_kernel(half, plan, *refs):
    *held, owned, away = refs
    z = lax.axis_index("row") // 2
    upper = (z >= half).astype(jnp.int32)
    distance = jnp.where(z >= half, z - half, half - 1 - z)
    for k in range(2):
        block = plan[3] + k
        block_upper = (block >= half).astype(jnp.int32)
        wanted = distance + half * jnp.abs(block_upper - upper)
        for d, blocks in enumerate(held):

            @pl.when(wanted == d)
            def _(blocks=blocks):
                owned[k] = blocks[block - half * block_upper]

    away[0] = owned[plan[0]]


def owned_section(plan, held):
    half, _, span = held[0].shape
    return pl.pallas_call(
        functools.partial(owned_kernel, half),
        in_specs=[smem()] + [vmem()] * len(held),
        out_specs=[vmem(), vmem()],
        out_shape=[
            jax.ShapeDtypeStruct((2, BLOCK, span), jnp.bfloat16),
            jax.ShapeDtypeStruct((1, BLOCK, span), jnp.bfloat16),
        ],
        compiler_params=params(),
        cost_estimate=cost(0, held[0].size * 12),
        name="owned_section",
    )(plan, *held)


def term_kernel(ys, keep, got, own, own_core, fix, fix_core, sent, kept):
    span = own.shape[2]
    right = jnp.concatenate(
        [
            own[...].reshape(2 * BLOCK, span),
            fix[0],
            own_core[...].reshape(2 * BLOCK, span),
            fix_core[0],
        ],
        axis=0,
    )
    for d in range(ys - 1, -1, -1):
        left = jnp.concatenate([keep[d], got[d]], axis=1)
        made = jnp.dot(left, right, preferred_element_type=jnp.float32)
        if d:
            sent[d - 1] = made.astype(jnp.bfloat16)
        else:
            kept[...] = made


def term_section(keep, got, own, own_core, fix, fix_core):
    ys = keep.shape[0]
    span = own.shape[2]
    return pl.pallas_call(
        functools.partial(term_kernel, ys),
        in_specs=[vmem()] * 6,
        out_specs=[vmem(), vmem()],
        out_shape=[
            jax.ShapeDtypeStruct((ys - 1, QB_DEV * BLOCK, span), jnp.bfloat16),
            jax.ShapeDtypeStruct((QB_DEV * BLOCK, span), jnp.float32),
        ],
        compiler_params=params(),
        cost_estimate=cost(2 * ys * QB_DEV * BLOCK * 6 * BLOCK * span, keep.size * 4 + span * BLOCK * 24),
        name="term_section",
    )(keep, got, own, own_core, fix, fix_core)


def per_device(
    coeff, tri_blocks, pair_aux, pair_ao, owner_slot, metric_blocks, pair_slot, pair_out
):
    rows = lax.axis_size("row")
    cols = lax.axis_size("col")
    pairs, ys = rows // 2, cols // 2

    def on_line(moves):
        return [(2 * a + x, 2 * b + x) for a, b in moves for x in range(2)]

    swap_pair = [(r, r ^ 1) for r in range(rows)]
    swap_core = [(c, c ^ 1) for c in range(cols)]

    *early, plan, left = first_section(tri_blocks, pair_aux, pair_ao, owner_slot, coeff, rows)
    made = (*early, *later_section(left, coeff))
    keep, send = metric_section(plan, pair_slot, pair_out, metric_blocks, cols)
    got = lax.ppermute(send, "col", swap_core)

    half = pairs // 2
    near_moves = [[(half - 1 - e, half - 1), (half + e, half)] for e in range(1, half)]
    far_moves = [[(half - 1 - e, half), (half + e, half - 1)] for e in range(half)]
    inward = [on_line(m) for m in near_moves], [on_line(m) for m in far_moves]
    beyond = pairs - (pairs - half) // 2 - half
    outward = [on_line([(b, a) for a, b in m]) for m in near_moves] + [
        on_line([(half - 1, half + e), (half, half - 1 - e)]) for e in range(beyond)
    ]
    around = [
        [(2 * y + k, 2 * ((y + d) % ys) + k) for y in range(ys) for k in range(2)] for d in range(1, ys)
    ]

    state = [{"came": [lax.ppermute(made[2 * p + 1], "row", swap_pair)]} for p in range(NUW)]
    moves_in = [*inward[1], *inward[0]]

    def pair(p, now):
        near, far = pair_section(made[2 * p], *now["came"])
        sources = [far] * half + [near] * (half - 1)
        order = (2, 0, 1) if len(moves_in) == len((2, 0, 1)) else range(len(moves_in))
        now["near"] = near
        now["came"] = [lax.ppermute(sources[k], "row", moves_in[k]) for k in order]
        return near

    def line(p, now):
        now["host"] = line_section([now["near"], *now["came"]])
        now["came"] = [lax.ppermute(now["host"], "row", m) for m in outward]
        return now["host"]

    def owned(p, now):
        now["own"], away = owned_section(plan, [now["host"], *now["came"]])
        now["came"] = [lax.ppermute(away, "row", swap_pair)]
        now["own_core"] = lax.ppermute(now["own"], "col", swap_core)
        return away

    def term(p, now):
        (fix,) = now["came"]
        fix_core = lax.ppermute(fix, "col", swap_core)
        sent, now["kept"] = term_section(keep, got, now["own"], now["own_core"], fix, fix_core)
        now["came"] = [lax.ppermute(sent[d - 1], "col", around[d - 1]) for d in range(1, ys)]
        return now["kept"]

    def finish(p, now):
        for part in now["came"]:
            now["kept"] = now["kept"] + part.astype(jnp.float32)
        now["kept"] = now["kept"].astype(jnp.bfloat16)
        return now["kept"]

    stages = [pair, line, owned, term, finish]
    order = ((0, 0), (0, 1), (1, 0), (2, 0), (3, 0), (4, 0), (1, 1), (2, 1), (3, 1), (4, 1))
    after = {(1, 0): [(0, 1)], (2, 0): [(0, 1)]}
    token = {}
    for index, p in order:
        now = state[p]
        if (index, p) in after:
            gated = lax.optimization_barrier((*now["came"], *[token[t] for t in after[index, p]]))
            now["came"] = list(gated[: len(now["came"])])
        token[index, p] = stages[index](p, now)
    return jnp.concatenate([now["kept"] for now in state], axis=1)


def solution(mesh):
    in_specs = (
        P("row", None),
        P(("row", "col"), None, None),
        P(("row", "col")),
        P(("row", "col")),
        P("col", None),
        P(("row", "col"), None, None),
        P(("row", "col")),
        P(("row", "col")),
    )
    out_specs = P(("row", "col"), None)
    return jax.shard_map(
        per_device, mesh=mesh, in_specs=in_specs, out_specs=out_specs, check_vma=False
    )
```
